1024 devices in a mesh: role: 2 (over y_hi), dp: 64 (over z, y_lo), tp: 8 (over x, core).
Axes of the slice: x: 4, y: 4 (y_hi: 2, y_lo: 2; y = y_hi * 2 + y_lo), z: 32, core: 2. Of those that a mesh axis runs over, the one named last changes fastest.
Arguments:
- hidden: bfloat16 [2, 8192, 8192], P('role', 'dp'), may hold values from -16 to 16
- out_grad: bfloat16 [8192, 1024], P('dp', 'tp'), may hold values from -6 to 6
- master: float32 [8192, 1024], P('dp', 'tp'), may hold values from -0.0625 to 0.0625
- moment1: float32 [8192, 1024], P('dp', 'tp'), may hold values from -18 to 18
- moment2: float32 [8192, 1024], P('dp', 'tp'), may hold values from 50 to 500
- queries: bfloat16 [8, 1024, 8192], P(None, 'dp', 'tp'), may hold values from -160 to 160
- new_keys: bfloat16 [8, 1024, 1024], P(None, 'dp', 'tp'), may hold values from -6 to 6
- k_cache: bfloat16 [1024, 256, 1024], P('dp', None, 'tp'), may hold values from -6 to 6
- v_cache: bfloat16 [1024, 256, 1024], P('dp', None, 'tp'), may hold values from -6 to 6
- cache_len: int32 [1024], P('dp'), may hold values from 2 to 256, as said below
Outputs:
- row_result: bfloat16 [2, 8192, 8192], P('role', 'dp', 'tp')
The draws below stay inside these ranges and needn't reach their ends.
Inputs may be any that keep to these rules, and one draw needn't show every extreme that they name: `cache_len`: some row holds exactly 256 cached positions.
All inputs are finite; a program needn't handle non-finite values.
Results may differ from the reference program's by a relative error of at most 0.008.
Values may be sent and summed in bfloat16 or wider, within the bound.
No kernel may reach another device: no remote copies, remote signals or barrier semaphores. Data moves between devices by JAX's collectives and lax.ppermute only.
A program may use at most 32 MiB of HBM per device.

```python
import math
import jax
import jax.numpy as jnp
from jax import lax

D = 8192
KVH = 8
QH = 64
HD = 128
STEPS = 8
ROWS_DEV = 16
CACHE = 256
TOKENS = 8192
ROWS = 1024
KVW = 1024
N_DP = 64
N_TP = 8


def shared_draw(key):
    base = jax.random.fold_in(key, 7)
    cache_keys = jnp.clip(jax.random.normal(jax.random.fold_in(base, 1), (ROWS, CACHE, KVH * HD), jnp.float32), -5.0, 5.0)
    query_vals = jnp.clip(2.0 * jax.random.normal(jax.random.fold_in(base, 2), (STEPS, ROWS, QH * HD), jnp.float32), -10.0, 10.0)
    return (query_vals, cache_keys)


def draw_queries(key, part):
    return shared_draw(key)[0].astype(jnp.bfloat16)


def draw_k_cache(key, part):
    return shared_draw(key)[1].astype(jnp.bfloat16)


def draw_cache_len(key, part):
    base = jax.random.fold_in(key, 31)
    wide_lengths = jax.random.randint(base, (ROWS,), 2, CACHE + 1, dtype=jnp.int32)
    short_top = max(CACHE // 8, 4)
    short_lengths = jax.random.randint(jax.random.fold_in(base, 2), (ROWS,), 2, short_top + 1, dtype=jnp.int32)
    picker = jax.random.randint(jax.random.fold_in(base, 3), (ROWS,), 0, 4, dtype=jnp.int32)
    lengths = jnp.where(picker == 0, wide_lengths, short_lengths)
    target = jax.random.randint(jax.random.fold_in(base, 1), (), 0, ROWS, dtype=jnp.int32)
    return lengths.at[target].set(CACHE)


def raised(values, rng, source, target, blocks, factor):
    def block_of(axis_at):
        return (jnp.arange(values.shape[axis_at]) // (values.shape[axis_at] // blocks)).reshape((-1,) + (1,) * (values.ndim - 1 - axis_at))

    near = jax.random.permutation(rng, blocks)[block_of(target)]
    other_side = (block_of(target) + blocks // 2) % blocks
    return jnp.where((block_of(source) == near) | (block_of(source) == other_side), factor * values, values)


def block_scale(rng, dims, pieces, low, largest):
    factor_of = 1.0
    for axis_at, blocks in pieces:
        steps = jax.random.uniform(jax.random.fold_in(jax.random.fold_in(rng, 6), axis_at), (blocks,), jnp.float32, low / len(pieces), largest / len(pieces))
        factor_of = factor_of * jnp.repeat(jnp.exp(steps), dims[axis_at] // blocks).reshape((-1,) + (1,) * (len(dims) - 1 - axis_at))
    return factor_of


def scatter_about(rng, extent, scale, most, shards=(), held_as=jnp.bfloat16):
    array = scale * jax.random.normal(rng, extent, jnp.float32)
    if shards:
        array = array * block_scale(rng, extent, shards, -0.22, 0.18)
    return jnp.clip(array, -most, most).astype(held_as)


def heavy_noise(stream_key, dims, scale, most, shards, heavy, kind=jnp.bfloat16):
    array = scale * jax.random.normal(stream_key, dims, jnp.float32)
    if shards:
        array = array * block_scale(stream_key, dims, shards, -0.22, 0.18)
    return jnp.clip(raised(array, jax.random.fold_in(stream_key, 3), *heavy), -most, most).astype(kind)


def setup_inputs(seed: int = 0) -> dict:
    seeds = jax.random.split(jax.random.key(seed), 11)
    hidden = heavy_noise(seeds[0], (2, TOKENS, D), 1.0, 16.0, ((0, 2), (1, 64)), (1, 2, 64, 4.0))
    out_grad = scatter_about(seeds[1], (TOKENS, KVW), 1.0, 6.0, ((0, 64), (1, 8)))
    master = scatter_about(seeds[2], (D, KVW), D ** -0.5, 0.0625, ((0, 64), (1, 8)), jnp.float32)
    moment1 = scatter_about(seeds[3], (D, KVW), 3.0, 18.0, ((0, 64), (1, 8)), jnp.float32)
    moment2 = jnp.clip(jnp.exp(math.log(500.0) - 2.3025851 * jax.random.uniform(seeds[4], (D, KVW), jnp.float32) ** block_scale(seeds[4], (D, KVW), ((0, 64), (1, 8)), -0.2, 0.2)), 50.0, 500.0)
    queries = draw_queries(jax.random.fold_in(seeds[10], 71), 0)
    new_keys = scatter_about(seeds[6], (STEPS, ROWS, KVW), 1.0, 6.0, ((1, 64), (2, 8)))
    k_cache = draw_k_cache(jax.random.fold_in(seeds[10], 71), 0)
    v_cache = scatter_about(seeds[8], (ROWS, CACHE, KVW), 1.0, 6.0, ((0, 64), (2, 8)))
    cache_len = draw_cache_len(jax.random.fold_in(seeds[10], 71), 0)
    return dict(hidden=hidden, out_grad=out_grad, master=master, moment1=moment1, moment2=moment2, queries=queries, new_keys=new_keys, k_cache=k_cache, v_cache=v_cache, cache_len=cache_len)


beta_one = 0.9
beta_two = 0.95
adam_eps = 1e-08
bias_one = 1.0 - 0.9 ** 10
bias_two = 1.0 - 0.95 ** 10
neg_fill = -1e+30

def adam_fresh(master, moment1, moment2, gradient):
    step_size = 2.0 * D ** (-0.5)
    first = beta_one * moment1 + (1.0 - beta_one) * gradient
    second = beta_two * moment2 + (1.0 - beta_two) * gradient * gradient
    change = first / bias_one / (jnp.sqrt(second / bias_two) + adam_eps)
    return (master - step_size * change).astype(jnp.bfloat16)

def attend_row(query_row, newkey_row, value_row, cache_keys, cache_vals, length):
    scale = HD ** (-0.5)
    cache_score = jnp.einsum('skgd,pkd->skgp', query_row.astype(jnp.float32), cache_keys.astype(jnp.float32)) * scale
    valid = jnp.arange(CACHE) < length
    cache_score = jnp.where(valid[None, None, None, :], cache_score, neg_fill)
    fresh_score = jnp.einsum('skgd,tkd->skgt', query_row.astype(jnp.float32), newkey_row.astype(jnp.float32)) * scale
    causal = jnp.arange(STEPS)[:, None] >= jnp.arange(STEPS)[None, :]
    fresh_score = jnp.where(causal[:, None, None, :], fresh_score, neg_fill)
    top = jnp.maximum(lax.optimization_barrier(jnp.max(cache_score, axis=-1)), lax.optimization_barrier(jnp.max(fresh_score, axis=-1)))
    cache_exp = jnp.exp(cache_score - top[..., None])
    fresh_exp = jnp.exp(fresh_score - top[..., None])
    total = lax.optimization_barrier(jnp.sum(cache_exp, axis=-1)) + lax.optimization_barrier(jnp.sum(fresh_exp, axis=-1))
    cache_wts = (cache_exp / total[..., None]).astype(jnp.bfloat16)
    fresh_wts = (fresh_exp / total[..., None]).astype(jnp.bfloat16)
    output = jnp.einsum('skgp,pkd->skgd', cache_wts.astype(jnp.float32), cache_vals.astype(jnp.float32))
    output = output + jnp.einsum('skgt,tkd->skgd', fresh_wts.astype(jnp.float32), value_row.astype(jnp.float32))
    return output.astype(jnp.bfloat16)

def reference(hidden, out_grad, master, moment1, moment2, queries, new_keys, k_cache, v_cache, cache_len):
    learn_in = hidden[0]
    roll_in = hidden[1]
    old_weight = master.astype(jnp.bfloat16)
    gradient = lax.dot_general(learn_in, out_grad, (((0,), (0,)), ((), ())), preferred_element_type=jnp.float32)
    span = KVH * HD // N_TP
    back_sum = jnp.zeros((TOKENS, D), jnp.float32)
    for group in range(N_TP):
        partial_value = jnp.dot(out_grad[:, group * span:(group + 1) * span], old_weight[:, group * span:(group + 1) * span].T, preferred_element_type=jnp.float32).astype(jnp.bfloat16)
        partial_value = lax.optimization_barrier(partial_value)
        back_sum = back_sum + partial_value.astype(jnp.float32)
    back_rows = back_sum.astype(jnp.bfloat16)
    fresh = adam_fresh(master, moment1, moment2, gradient)
    values = jnp.dot(roll_in, fresh, preferred_element_type=jnp.float32).astype(jnp.bfloat16)
    values = values.reshape(N_DP, STEPS, ROWS_DEV, KVH, HD).transpose(0, 2, 1, 3, 4).reshape(ROWS, STEPS, KVH, HD)
    query_all = queries.reshape(STEPS, ROWS, KVH, QH // KVH, HD).transpose(1, 0, 2, 3, 4)
    newkey_all = new_keys.reshape(STEPS, ROWS, KVH, HD).transpose(1, 0, 2, 3)
    cache_keys = k_cache.reshape(ROWS, CACHE, KVH, HD)
    cache_vals = v_cache.reshape(ROWS, CACHE, KVH, HD)

    def one_row(packed):
        return attend_row(packed[0], packed[1], packed[2], packed[3], packed[4], packed[5])
    attended = lax.map(one_row, (query_all, newkey_all, values, cache_keys, cache_vals, cache_len))
    attended = attended.reshape(N_DP, ROWS_DEV, STEPS, D).transpose(0, 2, 1, 3).reshape(TOKENS, D)
    return jnp.stack([back_rows, attended])
```

```python
import jax
import jax.numpy as jnp
from jax import lax
from jax.sharding import Mesh, PartitionSpec as P

D = 8192
KVH = 8
QH = 64
HD = 128
STEPS = 8


beta_one = 0.9
beta_two = 0.95
adam_eps = 1e-08
bias_one = 1.0 - 0.9**10
bias_two = 1.0 - 0.95**10
neg_fill = -1e30

DP = ("zh", "zl", "yl")
TP = ("x", "core")
NEAR = ("zl", "yl")


def adam_fresh(master, moment1, moment2, gradient):
    step_size = 2.0 * D ** (-0.5)
    first = beta_one * moment1 + (1.0 - beta_one) * gradient
    second = beta_two * moment2 + (1.0 - beta_two) * gradient * gradient
    change = first / bias_one / (jnp.sqrt(second / bias_two) + adam_eps)
    return (master - step_size * change).astype(jnp.bfloat16)


def exchange(value, axis):
    return lax.all_to_all(value, axis, 0, 0, tiled=True)


def gather(value, axis):
    peers = lax.axis_size(axis)
    return exchange(jnp.broadcast_to(value[None], (peers, *value.shape)), axis)


def swap_core(value):
    return lax.ppermute(value, "core", [(0, 1), (1, 0)])


def dot32(a, b, dims):
    return lax.dot_general(a, b, (dims, ((), ())), preferred_element_type=jnp.float32)


def local(
    hidden, out_grad, master, moment1, moment2, queries, new_keys, k_cache, v_cache, cache_len
):
    is_learner = lax.axis_index("role") == 0
    x_at = lax.axis_index("x")
    core_at = lax.axis_index("core")
    far, near = lax.axis_size("zh"), lax.axis_size("zl") * lax.axis_size("yl")
    tokens, block = hidden.shape[1], master.shape[0]
    half = tokens // 2
    width_here = out_grad.shape[1]
    heads_here = width_here // HD
    share = QH // KVH
    replica_rows = cache_len.shape[0]
    cache_size = k_cache.shape[1]

    mine = lax.dynamic_slice(hidden[0], (core_at * half, x_at * near * block), (half, near * block))
    mine = mine.reshape(half, near, block).transpose(1, 0, 2)
    mine = exchange(mine, NEAR)
    mine = gather(mine.reshape(near * half, block), "x")
    other = swap_core(mine)

    grads = gather(out_grad, "zl")
    grads = jnp.stack(yl_pair(grads), axis=1)
    grads = grads.reshape(near, tokens, width_here)
    at_mine = lax.dynamic_slice(grads, (0, core_at * half, 0), (near, half, width_here))
    at_other = lax.dynamic_slice(grads, (0, (1 - core_at) * half, 0), (near, half, width_here))
    at_mine = at_mine.reshape(near * half, width_here)
    at_other = at_other.reshape(near * half, width_here)

    partial = jnp.stack(
        [
            dot32(mine[f], at_mine, ((0,), (0,))) + dot32(other[f], at_other, ((0,), (0,)))
            for f in range(far)
        ]
    ).astype(jnp.bfloat16)
    gradient = jnp.sum(exchange(partial, "zh").astype(jnp.float32), axis=0)
    fresh = adam_fresh(master, moment1, moment2, gradient)

    old_weight = gather(master.astype(jnp.bfloat16), "zh")
    back = jnp.stack(
        [
            jnp.stack(
                [
                    dot32(rows, old_weight[f], ((1,), (1,))).astype(jnp.bfloat16)
                    for f in range(far)
                ]
            )
            for rows in (at_mine, at_other)
        ]
    )
    kept, sent = back[0], back[1]
    back = (kept.astype(jnp.float32) + swap_core(sent).astype(jnp.float32)).astype(jnp.bfloat16)
    back = jnp.sum(exchange(back, "x").astype(jnp.float32), axis=0).astype(jnp.bfloat16)
    back = exchange(back.reshape(near, half, block), NEAR)
    back = back.reshape(2, near // 2, half, block)
    stays = lax.dynamic_index_in_dim(back, core_at, 0, keepdims=False)
    leaves = lax.dynamic_index_in_dim(back, 1 - core_at, 0, keepdims=False)
    comes = swap_core(leaves)
    low = jnp.where(core_at == 0, stays, comes)
    high = jnp.where(core_at == 0, comes, stays)
    learner_rows = jnp.concatenate([low, high], axis=1).transpose(1, 0, 2)
    learner_rows = learner_rows.reshape(tokens, near // 2 * block)

    arrived = lax.ppermute(fresh, "role", [(0, 1)])
    weight = gather(arrived, "zh")
    new_mine = sum(dot32(mine[f], weight[f], ((1,), (0,))) for f in range(far))
    new_other = sum(dot32(other[f], weight[f], ((1,), (0,))) for f in range(far))
    new_mine = new_mine.astype(jnp.bfloat16).reshape(near, half, width_here)
    new_other = new_other.astype(jnp.bfloat16).reshape(near, half, width_here)
    low = jnp.where(core_at == 0, new_mine, new_other)
    high = jnp.where(core_at == 0, new_other, new_mine)
    values = exchange(jnp.concatenate([low, high], axis=1), NEAR)
    values = jnp.sum(values.astype(jnp.float32), axis=0)

    values = values.astype(jnp.bfloat16).reshape(STEPS, replica_rows, heads_here, HD)
    query_all = queries.reshape(STEPS, replica_rows, heads_here, share, HD)
    newkey_all = new_keys.reshape(STEPS, replica_rows, heads_here, HD)
    cache_keys = k_cache.reshape(replica_rows, cache_size, heads_here, HD)
    cache_vals = v_cache.reshape(replica_rows, cache_size, heads_here, HD)
    scale = HD ** (-0.5)
    cache_score = (
        jnp.einsum("srkgd,rpkd->srkgp", query_all, cache_keys, preferred_element_type=jnp.float32)
        * scale
    )
    valid = jnp.arange(cache_size)[None, :] < cache_len[:, None]
    cache_score = jnp.where(valid[None, :, None, None, :], cache_score, neg_fill)
    fresh_score = (
        jnp.einsum("srkgd,trkd->srkgt", query_all, newkey_all, preferred_element_type=jnp.float32)
        * scale
    )
    causal = jnp.arange(STEPS)[:, None] >= jnp.arange(STEPS)[None, :]
    fresh_score = jnp.where(causal[:, None, None, None, :], fresh_score, neg_fill)
    top = jnp.maximum(jnp.max(cache_score, axis=-1), jnp.max(fresh_score, axis=-1))
    cache_exp = jnp.exp(cache_score - top[..., None])
    fresh_exp = jnp.exp(fresh_score - top[..., None])
    total = jnp.sum(cache_exp, axis=-1) + jnp.sum(fresh_exp, axis=-1)
    cache_wts = (cache_exp / total[..., None]).astype(jnp.bfloat16)
    fresh_wts = (fresh_exp / total[..., None]).astype(jnp.bfloat16)
    output = jnp.einsum(
        "srkgp,rpkd->srkgd", cache_wts, cache_vals, preferred_element_type=jnp.float32
    )
    output = output + jnp.einsum(
        "srkgt,trkd->srkgd", fresh_wts, values, preferred_element_type=jnp.float32
    )
    decoded = output.astype(jnp.bfloat16).reshape(STEPS * replica_rows, heads_here * share * HD)
    result = jnp.where(is_learner, learner_rows, decoded)
    return result[None]


def yl_pair(value):
    met = lax.ppermute(value, "yl", [(0, 1), (1, 0)])
    first = lax.axis_index("yl") == 0
    return jnp.where(first, value, met), jnp.where(first, met, value)


def solution(mesh):
    roles, dp, tp = (mesh.shape[name] for name in ("role", "dp", "tp"))
    x_size = tp // 2
    fine = Mesh(
        mesh.devices.reshape(roles, x_size, dp // (2 * x_size), 2, x_size, 2),
        ("role", *DP, *TP),
    )
    return jax.shard_map(
        local,
        mesh=fine,
        in_specs=(
            P("role", DP, None),
            P(DP, TP),
            P(DP, TP),
            P(DP, TP),
            P(DP, TP),
            P(None, DP, TP),
            P(None, DP, TP),
            P(DP, None, TP),
            P(DP, None, TP),
            P(DP),
        ),
        out_specs=P("role", DP, TP),
        check_vma=False,
    )
```

```python
import jax
import jax.numpy as jnp
from jax import lax
from jax.sharding import Mesh, PartitionSpec as P

D = 8192
KVH = 8
QH = 64
HD = 128
STEPS = 8


beta_one = 0.9
beta_two = 0.95
adam_eps = 1e-08
bias_one = 1.0 - 0.9**10
bias_two = 1.0 - 0.95**10
neg_fill = -1e30

DP = ("zh", "zl", "yl")
TP = ("x", "core")
NEAR = ("zl", "yl")


def adam_fresh(master, moment1, moment2, gradient):
    step_size = 2.0 * D ** (-0.5)
    first = beta_one * moment1 + (1.0 - beta_one) * gradient
    second = beta_two * moment2 + (1.0 - beta_two) * gradient * gradient
    change = first / bias_one / (jnp.sqrt(second / bias_two) + adam_eps)
    return (master - step_size * change).astype(jnp.bfloat16)


def exchange(value, axis):
    return lax.all_to_all(value, axis, 0, 0, tiled=True)


def gather(value, axis):
    peers = lax.axis_size(axis)
    return exchange(jnp.broadcast_to(value[None], (peers, *value.shape)), axis)


def swap(value, axis, by=1):
    peers = lax.axis_size(axis)
    return lax.ppermute(value, axis, [(i, i ^ by) for i in range(peers)])


def ordered(value, met, first):
    return jnp.where(first, value, met), jnp.where(first, met, value)


def doubled(value, axis):
    by, at = lax.axis_size(axis) // 2, 0
    while by:
        first = lax.axis_index(axis) & by == 0
        value = jnp.stack(ordered(value, swap(value, axis, by), first), axis=at)
        by, at = by // 2, at + 1
    return value, at


def far_shift(value, by, to_role):
    far = lax.axis_size("zh")
    pairs = [(i, to_role * far + (i + by) % far) for i in range(far)]
    return lax.ppermute(value, ("role", "zh"), pairs)


def far_order(far):
    return sorted(range(far), key=lambda k: -min(k, far - k))


def by_source(received):
    far = len(received)
    back = [received[-m % far] for m in range(far)]
    return lax.dynamic_slice_in_dim(jnp.stack(back + back), -lax.axis_index("zh") % far, far, 0)


def at_index(value, index):
    return lax.dynamic_index_in_dim(value, index, 0, keepdims=False)


def dot32(a, b, dims):
    return lax.dot_general(a, b, (dims, ((), ())), preferred_element_type=jnp.float32)


def local(
    hidden, out_grad, master, moment1, moment2, queries, new_keys, k_cache, v_cache, cache_len
):
    is_learner = lax.axis_index("role") == 0
    x_at, core_at = lax.axis_index("x"), lax.axis_index("core")
    zh_at, yl_at = lax.axis_index("zh"), lax.axis_index("yl")
    far, line = lax.axis_size("zh"), lax.axis_size("zl")
    near = line * 2
    tokens, block = hidden.shape[1], master.shape[0]
    half = tokens // 2
    width_here = out_grad.shape[1]
    heads_here = width_here // HD
    share = QH // KVH
    replica_rows = cache_len.shape[0]
    cache_size = k_cache.shape[1]

    mine = lax.dynamic_slice(hidden[0], (core_at * half, x_at * near * block), (half, near * block))
    mine = mine.reshape(half, near, block).transpose(1, 0, 2)
    mine = exchange(mine, NEAR)
    mine = gather(mine.reshape(near * half, block), "x")
    other = swap(mine, "core")

    grads, at = doubled(out_grad, "zl")
    grads = jnp.stack(ordered(grads, swap(grads, "yl"), yl_at == 0), axis=at)
    grads = grads.reshape(near, tokens, width_here)
    rows_at = [lax.dynamic_slice(grads, (0, at * half, 0), (near, half, width_here)) for at in (core_at, 1 - core_at)]
    at_mine, at_other = (rows.reshape(near * half, width_here) for rows in rows_at)

    old_weight = master.astype(jnp.bfloat16)
    old_parts = {k: far_shift(old_weight, k, 0) for k in far_order(far)[:-1]}
    old_parts[0] = old_weight
    old_weight = by_source([old_parts[k] for k in range(far)])
    kept, sent = (
        jnp.stack([dot32(rows, old_weight[f], ((1,), (1,))).astype(jnp.bfloat16) for f in range(far)])
        for rows in (at_mine, at_other)
    )
    sent_back = (kept.astype(jnp.float32) + swap(sent, "core").astype(jnp.float32)).astype(jnp.bfloat16)

    partial = jnp.stack(
        [
            dot32(mine[f], at_mine, ((0,), (0,))) + dot32(other[f], at_other, ((0,), (0,)))
            for f in range(far)
        ]
    )
    gradient = at_index(partial, zh_at)
    narrow, sent_back = lax.optimization_barrier((partial.astype(jnp.bfloat16), sent_back))
    for k in far_order(far)[:-1]:
        gradient += far_shift(at_index(narrow, (zh_at + k) % far), k, 0).astype(jnp.float32)
    fresh = adam_fresh(master, moment1, moment2, gradient)

    back = jnp.sum(exchange(sent_back, "x").astype(jnp.float32), axis=0).astype(jnp.bfloat16)
    back = back.reshape(line, 2, half, block)
    stays = lax.dynamic_index_in_dim(back, yl_at, 1, keepdims=False)
    leaves = lax.dynamic_index_in_dim(back, 1 - yl_at, 1, keepdims=False)
    back = jnp.stack(ordered(stays, swap(leaves, "yl"), yl_at == 0), axis=1)

    parts = {k: far_shift(fresh, k, 1) for k in far_order(far)}
    weight = by_source([parts[k] for k in range(far)])
    terms = [sum(dot32(rows[f], weight[f], ((1,), (0,))) for f in range(far)) for rows in (mine, other)]
    terms = jnp.stack([rows.reshape(line, 2, half, width_here) for rows in terms], axis=2)
    stays = lax.dynamic_index_in_dim(terms, yl_at, 1, keepdims=False)
    leaves = lax.dynamic_index_in_dim(terms, 1 - yl_at, 1, keepdims=False)
    terms = stays + swap(leaves.astype(jnp.bfloat16), "yl").astype(jnp.float32)

    moved = exchange(jnp.where(is_learner, back, terms.astype(jnp.bfloat16)), "zl")
    values = jnp.sum(moved.astype(jnp.float32), axis=0)
    values = jnp.concatenate(ordered(values[0], values[1], core_at == 0))
    back = moved.reshape(2, near // 2, half, block)
    stays, leaves = at_index(back, core_at), at_index(back, 1 - core_at)
    learner_rows = jnp.concatenate(ordered(stays, swap(leaves, "core"), core_at == 0), axis=1)
    learner_rows = learner_rows.transpose(1, 0, 2).reshape(tokens, near // 2 * block)

    values = values.astype(jnp.bfloat16).reshape(STEPS, replica_rows, heads_here, HD)
    query_all = queries.reshape(STEPS, replica_rows, heads_here, share, HD)
    newkey_all = new_keys.reshape(STEPS, replica_rows, heads_here, HD)
    cache_keys = k_cache.reshape(replica_rows, cache_size, heads_here, HD)
    cache_vals = v_cache.reshape(replica_rows, cache_size, heads_here, HD)
    scale = HD ** (-0.5)
    cache_score = (
        jnp.einsum("srkgd,rpkd->srkgp", query_all, cache_keys, preferred_element_type=jnp.float32)
        * scale
    )
    valid = jnp.arange(cache_size)[None, :] < cache_len[:, None]
    cache_score = jnp.where(valid[None, :, None, None, :], cache_score, neg_fill)
    fresh_score = (
        jnp.einsum("srkgd,trkd->srkgt", query_all, newkey_all, preferred_element_type=jnp.float32)
        * scale
    )
    causal = jnp.arange(STEPS)[:, None] >= jnp.arange(STEPS)[None, :]
    fresh_score = jnp.where(causal[:, None, None, None, :], fresh_score, neg_fill)
    top = jnp.maximum(jnp.max(cache_score, axis=-1), jnp.max(fresh_score, axis=-1))
    cache_exp = jnp.exp(cache_score - top[..., None])
    fresh_exp = jnp.exp(fresh_score - top[..., None])
    total = jnp.sum(cache_exp, axis=-1) + jnp.sum(fresh_exp, axis=-1)
    cache_wts = (cache_exp / total[..., None]).astype(jnp.bfloat16)
    fresh_wts = (fresh_exp / total[..., None]).astype(jnp.bfloat16)
    output = jnp.einsum(
        "srkgp,rpkd->srkgd", cache_wts, cache_vals, preferred_element_type=jnp.float32
    )
    output = output + jnp.einsum(
        "srkgt,trkd->srkgd", fresh_wts, values, preferred_element_type=jnp.float32
    )
    decoded = output.astype(jnp.bfloat16).reshape(STEPS * replica_rows, heads_here * share * HD)
    result = jnp.where(is_learner, learner_rows, decoded)
    return result[None]


def solution(mesh):
    roles, dp, tp = (mesh.shape[name] for name in ("role", "dp", "tp"))
    x_size = tp // 2
    fine = Mesh(
        mesh.devices.reshape(roles, x_size, dp // (2 * x_size), 2, x_size, 2),
        ("role", *DP, *TP),
    )
    return jax.shard_map(
        local,
        mesh=fine,
        in_specs=(
            P("role", DP, None),
            P(DP, TP),
            P(DP, TP),
            P(DP, TP),
            P(DP, TP),
            P(None, DP, TP),
            P(None, DP, TP),
            P(DP, None, TP),
            P(DP, None, TP),
            P(DP),
        ),
        out_specs=P("role", DP, TP),
        check_vma=False,
    )
```

```python
import jax
import jax.numpy as jnp
from jax import lax
from jax.sharding import Mesh, PartitionSpec as P


D = 8192
KVH = 8
QH = 64
HD = 128
STEPS = 8


beta_one = 0.9
beta_two = 0.95
adam_eps = 1e-08
bias_one = 1.0 - 0.9**10
bias_two = 1.0 - 0.95**10
neg_fill = -1e30

DP = ("zh", "zl", "yl")
TP = ("x", "core")
NEAR = ("zl", "yl")


def adam_fresh(master, moment1, moment2, gradient):
    step_size = 2.0 * D ** (-0.5)
    first = beta_one * moment1 + (1.0 - beta_one) * gradient
    second = beta_two * moment2 + (1.0 - beta_two) * gradient * gradient
    change = first / bias_one / (jnp.sqrt(second / bias_two) + adam_eps)
    return (master - step_size * change).astype(jnp.bfloat16)


def exchange(value, axis):
    return lax.all_to_all(value, axis, 0, 0, tiled=True)


def gather(value, axis):
    peers = lax.axis_size(axis)
    return exchange(jnp.broadcast_to(value[None], (peers, *value.shape)), axis)


def swap(value, axis, by=1):
    peers = lax.axis_size(axis)
    return lax.ppermute(value, axis, [(i, i ^ by) for i in range(peers)])


def ordered(value, met, first):
    return jnp.where(first, value, met), jnp.where(first, met, value)


def far_shift(value, by, from_role, to_role):
    far = lax.axis_size("zh")
    pairs = [(from_role * far + i, to_role * far + (i + by) % far) for i in range(far)]
    return lax.ppermute(value, ("role", "zh"), pairs)


def far_order(far):
    return sorted(range(far), key=lambda k: -min(k, far - k))


def by_source(received):
    far = len(received)
    back = [received[-m % far] for m in range(far)]
    return lax.dynamic_slice_in_dim(jnp.stack(back + back), -lax.axis_index("zh") % far, far, 0)


def at_index(value, index):
    return lax.dynamic_index_in_dim(value, index, 0, keepdims=False)


def dot32(a, b, dims):
    return lax.dot_general(a, b, (dims, ((), ())), preferred_element_type=jnp.float32)


def local(
    hidden, out_grad, master, moment1, moment2, queries, new_keys, k_cache, v_cache, cache_len
):
    is_learner = lax.axis_index("role") == 0
    x_at, core_at = lax.axis_index("x"), lax.axis_index("core")
    zh_at, yl_at = lax.axis_index("zh"), lax.axis_index("yl")
    far, line = lax.axis_size("zh"), lax.axis_size("zl")
    near = line * 2
    tokens, block = hidden.shape[1], master.shape[0]
    half = tokens // 2
    width_here = out_grad.shape[1]
    heads_here = width_here // HD
    share = QH // KVH
    replica_rows = cache_len.shape[0]
    cache_size = k_cache.shape[1]

    mine = lax.dynamic_slice(hidden[0], (core_at * half, x_at * near * block), (half, near * block))
    mine = mine.reshape(half, near, block).transpose(1, 0, 2)
    mine = exchange(mine, NEAR)

    by, grads, at = line // 2, out_grad, 0
    while by:
        first = lax.axis_index("zl") & by == 0
        grads = jnp.stack(ordered(grads, swap(grads, "zl", by), first), axis=at)
        if at == 0:
            grads, mine = lax.optimization_barrier((grads, mine))
        by, at = by // 2, at + 1
    grads = jnp.stack(ordered(grads, swap(grads, "yl"), yl_at == 0), axis=at)
    grads = grads.reshape(near, tokens, width_here)
    at_mine, at_other = (
        lax.dynamic_slice(grads, (0, at * half, 0), (near, half, width_here)).reshape(near * half, width_here)
        for at in (core_at, 1 - core_at)
    )

    mine = gather(mine.reshape(near * half, block), "x")
    other = swap(mine, "core")

    partial = jnp.stack(
        [
            dot32(mine[f], at_mine, ((0,), (0,))) + dot32(other[f], at_other, ((0,), (0,)))
            for f in range(far)
        ]
    ).astype(jnp.bfloat16)
    partial, old_weight = lax.optimization_barrier((partial, master.astype(jnp.bfloat16)))
    gradient = [far_shift(at_index(partial, (zh_at + k) % far), k, 0, 1) for k in far_order(far)]

    old_parts = {k: far_shift(old_weight, k, 0, 0) for k in far_order(far)[:-1]}
    old_parts[0] = old_weight
    old_weight = by_source([old_parts[k] for k in range(far)])
    kept, sent = (
        jnp.stack([dot32(rows, old_weight[f], ((1,), (1,))).astype(jnp.bfloat16) for f in range(far)])
        for rows in (at_mine, at_other)
    )
    back = (kept.astype(jnp.float32) + swap(sent, "core").astype(jnp.float32)).astype(jnp.bfloat16)
    gradient, back = lax.optimization_barrier((gradient, back))
    back = jnp.sum(exchange(back, "x").astype(jnp.float32), axis=0).astype(jnp.bfloat16)
    back = back.reshape(line, 2, half, block)
    stays = lax.dynamic_index_in_dim(back, yl_at, 1, keepdims=False)
    leaves = lax.dynamic_index_in_dim(back, 1 - yl_at, 1, keepdims=False)
    back = jnp.stack(ordered(stays, swap(leaves, "yl"), yl_at == 0), axis=1)

    fresh = adam_fresh(master, moment1, moment2, sum(g.astype(jnp.float32) for g in gradient))
    parts = {k: far_shift(fresh, k, 1, 1) for k in far_order(far)[:-1]}
    parts[0] = fresh
    weight = by_source([parts[k] for k in range(far)])
    terms = [sum(dot32(rows[f], weight[f], ((1,), (0,))) for f in range(far)) for rows in (mine, other)]
    terms = jnp.stack([rows.reshape(line, 2, half, width_here) for rows in terms], axis=2)
    stays = lax.dynamic_index_in_dim(terms, yl_at, 1, keepdims=False)
    leaves = lax.dynamic_index_in_dim(terms, 1 - yl_at, 1, keepdims=False)
    terms = stays + swap(leaves.astype(jnp.bfloat16), "yl").astype(jnp.float32)

    moved = exchange(jnp.where(is_learner, back, terms.astype(jnp.bfloat16)), "zl")
    values = jnp.sum(moved.astype(jnp.float32), axis=0)
    values = jnp.concatenate(ordered(values[0], values[1], core_at == 0))
    back = moved.reshape(2, near // 2, half, block)
    stays, leaves = at_index(back, core_at), at_index(back, 1 - core_at)
    learner_rows = jnp.concatenate(ordered(stays, swap(leaves, "core"), core_at == 0), axis=1)
    learner_rows = learner_rows.transpose(1, 0, 2).reshape(tokens, near // 2 * block)

    values = values.astype(jnp.bfloat16).reshape(STEPS, replica_rows, heads_here, HD)
    query_all = queries.reshape(STEPS, replica_rows, heads_here, share, HD)
    newkey_all = new_keys.reshape(STEPS, replica_rows, heads_here, HD)
    cache_keys = k_cache.reshape(replica_rows, cache_size, heads_here, HD)
    cache_vals = v_cache.reshape(replica_rows, cache_size, heads_here, HD)
    scale = HD ** (-0.5)
    cache_score = (
        jnp.einsum("srkgd,rpkd->srkgp", query_all, cache_keys, preferred_element_type=jnp.float32)
        * scale
    )
    valid = jnp.arange(cache_size)[None, :] < cache_len[:, None]
    cache_score = jnp.where(valid[None, :, None, None, :], cache_score, neg_fill)
    fresh_score = (
        jnp.einsum("srkgd,trkd->srkgt", query_all, newkey_all, preferred_element_type=jnp.float32)
        * scale
    )
    causal = jnp.arange(STEPS)[:, None] >= jnp.arange(STEPS)[None, :]
    fresh_score = jnp.where(causal[:, None, None, None, :], fresh_score, neg_fill)
    top = jnp.maximum(jnp.max(cache_score, axis=-1), jnp.max(fresh_score, axis=-1))
    cache_exp = jnp.exp(cache_score - top[..., None])
    fresh_exp = jnp.exp(fresh_score - top[..., None])
    total = jnp.sum(cache_exp, axis=-1) + jnp.sum(fresh_exp, axis=-1)
    cache_wts = (cache_exp / total[..., None]).astype(jnp.bfloat16)
    fresh_wts = (fresh_exp / total[..., None]).astype(jnp.bfloat16)
    output = jnp.einsum(
        "srkgp,rpkd->srkgd", cache_wts, cache_vals, preferred_element_type=jnp.float32
    )
    output = output + jnp.einsum(
        "srkgt,trkd->srkgd", fresh_wts, values, preferred_element_type=jnp.float32
    )
    decoded = output.astype(jnp.bfloat16).reshape(STEPS * replica_rows, heads_here * share * HD)
    result = jnp.where(is_learner, learner_rows, decoded)
    return result[None]


def solution(mesh):
    roles, dp, tp = (mesh.shape[name] for name in ("role", "dp", "tp"))
    x_size = tp // 2
    fine = Mesh(
        mesh.devices.reshape(roles, x_size, dp // (2 * x_size), 2, x_size, 2),
        ("role", *DP, *TP),
    )
    return jax.shard_map(
        local,
        mesh=fine,
        in_specs=(
            P("role", DP, None),
            P(DP, TP),
            P(DP, TP),
            P(DP, TP),
            P(DP, TP),
            P(None, DP, TP),
            P(None, DP, TP),
            P(DP, None, TP),
            P(DP, None, TP),
            P(DP),
        ),
        out_specs=P("role", DP, TP),
        check_vma=False,
    )
```

```python
import jax
import jax.numpy as jnp
from jax import lax
from jax.sharding import Mesh, PartitionSpec as P


D = 8192
KVH = 8
QH = 64
HD = 128
STEPS = 8


beta_one = 0.9
beta_two = 0.95
adam_eps = 1e-08
bias_one = 1.0 - 0.9**10
bias_two = 1.0 - 0.95**10
neg_fill = -1e30


DP = ("zh", "zl", "yl")
TP = ("x", "core")
NEAR = ("zl", "yl")


def adam_fresh(master, moment1, moment2, gradient):
    step_size = 2.0 * D ** (-0.5)
    first = beta_one * moment1 + (1.0 - beta_one) * gradient
    second = beta_two * moment2 + (1.0 - beta_two) * gradient * gradient
    change = first / bias_one / (jnp.sqrt(second / bias_two) + adam_eps)
    return (master - step_size * change).astype(jnp.bfloat16)


def exchange(value, axis):
    return lax.all_to_all(value, axis, 0, 0, tiled=True)


def gather(value, axis):
    peers = lax.axis_size(axis)
    return exchange(jnp.broadcast_to(value[None], (peers, *value.shape)), axis)


def swap(value, axis, by=1):
    peers = lax.axis_size(axis)
    return lax.ppermute(value, axis, [(i, i ^ by) for i in range(peers)])


def ordered(value, met, first):
    return jnp.where(first, value, met), jnp.where(first, met, value)


def far_shift(value, by, from_role, to_role):
    far = lax.axis_size("zh")
    pairs = [(from_role * far + i, to_role * far + (i + by) % far) for i in range(far)]
    return lax.ppermute(value, ("role", "zh"), pairs)


def far_order(far):
    return sorted(range(far), key=lambda k: -min(k, far - k))


def by_source(received):
    far = len(received)
    back = [received[-m % far] for m in range(far)]
    return lax.dynamic_slice_in_dim(jnp.stack(back + back), -lax.axis_index("zh") % far, far, 0)


def at_index(value, index):
    return lax.dynamic_index_in_dim(value, index, 0, keepdims=False)


def dot32(a, b, dims):
    return lax.dot_general(a, b, (dims, ((), ())), preferred_element_type=jnp.float32)


def local(
    hidden, out_grad, master, moment1, moment2, queries, new_keys, k_cache, v_cache, cache_len
):
    is_learner = lax.axis_index("role") == 0
    x_at, core_at = lax.axis_index("x"), lax.axis_index("core")
    zh_at, yl_at = lax.axis_index("zh"), lax.axis_index("yl")
    far, line = lax.axis_size("zh"), lax.axis_size("zl")
    near = line * 2
    tokens, block = hidden.shape[1], master.shape[0]
    half = tokens // 2
    width_here = out_grad.shape[1]
    heads_here = width_here // HD
    share = QH // KVH
    replica_rows = cache_len.shape[0]
    cache_size = k_cache.shape[1]

    mine = lax.dynamic_slice(hidden[0], (core_at * half, x_at * near * block), (half, near * block))
    mine = mine.reshape(half, near, block).transpose(1, 0, 2)
    mine = exchange(mine, NEAR)

    by, grads, at = line // 2, out_grad, 0
    while by:
        first = lax.axis_index("zl") & by == 0
        grads = jnp.stack(ordered(grads, swap(grads, "zl", by), first), axis=at)
        if at == 0:
            grads, mine = lax.optimization_barrier((grads, mine))
        by, at = by // 2, at + 1
    grads = jnp.stack(ordered(grads, swap(grads, "yl"), yl_at == 0), axis=at)
    grads = grads.reshape(near, tokens, width_here)
    at_mine, at_other = (
        lax.dynamic_slice(grads, (0, at * half, 0), (near, half, width_here)).reshape(near * half, width_here)
        for at in (core_at, 1 - core_at)
    )

    mine, old_weight = lax.optimization_barrier((mine, master.astype(jnp.bfloat16)))
    mine = gather(mine.reshape(near * half, block), "x")
    other = swap(mine, "core")

    old_parts = {k: far_shift(old_weight, k, 1, 0) for k in far_order(far)[:-1]}
    old_parts[0] = old_weight

    partial = jnp.stack(
        [
            dot32(mine[f], at_mine, ((0,), (0,))) + dot32(other[f], at_other, ((0,), (0,)))
            for f in range(far)
        ]
    ).astype(jnp.bfloat16)
    gradient = [at_index(partial, zh_at)] + [
        far_shift(at_index(partial, (zh_at + k) % far), k, 0, 0)
        for k in far_order(far)[:-1]
    ]

    _, *old_parts = lax.optimization_barrier((partial, *(old_parts[k] for k in range(far))))
    old_weight = by_source(old_parts)
    kept, sent = (
        jnp.stack([dot32(rows, old_weight[f], ((1,), (1,))).astype(jnp.bfloat16) for f in range(far)])
        for rows in (at_mine, at_other)
    )
    back = (kept.astype(jnp.float32) + swap(sent, "core").astype(jnp.float32)).astype(jnp.bfloat16)
    gradient, back = lax.optimization_barrier((gradient, back))

    fresh = adam_fresh(master, moment1, moment2, sum(g.astype(jnp.float32) for g in gradient))
    parts = {k: far_shift(fresh, k, 0, 1) for k in far_order(far)}
    parts = [parts[k] for k in range(far)]

    back = exchange(back, "x")
    back = jnp.sum(back.astype(jnp.float32), axis=0).astype(jnp.bfloat16)
    back = back.reshape(line, 2, half, block)
    stays = lax.dynamic_index_in_dim(back, yl_at, 1, keepdims=False)
    leaves = lax.dynamic_index_in_dim(back, 1 - yl_at, 1, keepdims=False)
    back = jnp.stack(ordered(stays, swap(leaves, "yl"), yl_at == 0), axis=1)

    parts, back = lax.optimization_barrier((parts, back))
    weight = by_source(parts)
    terms = [sum(dot32(rows[f], weight[f], ((1,), (0,))) for f in range(far)) for rows in (mine, other)]
    terms = jnp.stack([rows.reshape(line, 2, half, width_here) for rows in terms], axis=2)
    stays = lax.dynamic_index_in_dim(terms, yl_at, 1, keepdims=False)
    leaves = lax.dynamic_index_in_dim(terms, 1 - yl_at, 1, keepdims=False)
    terms = stays + swap(leaves.astype(jnp.bfloat16), "yl").astype(jnp.float32)

    moved = exchange(jnp.where(is_learner, back, terms.astype(jnp.bfloat16)), "zl")
    values = jnp.sum(moved.astype(jnp.float32), axis=0)
    values = jnp.concatenate(ordered(values[0], values[1], core_at == 0))
    back = moved.reshape(2, near // 2, half, block)
    stays, leaves = at_index(back, core_at), at_index(back, 1 - core_at)
    learner_rows = jnp.concatenate(ordered(stays, swap(leaves, "core"), core_at == 0), axis=1)
    learner_rows = learner_rows.transpose(1, 0, 2).reshape(tokens, near // 2 * block)

    values = values.astype(jnp.bfloat16).reshape(STEPS, replica_rows, heads_here, HD)
    query_all = queries.reshape(STEPS, replica_rows, heads_here, share, HD)
    newkey_all = new_keys.reshape(STEPS, replica_rows, heads_here, HD)
    cache_keys = k_cache.reshape(replica_rows, cache_size, heads_here, HD)
    cache_vals = v_cache.reshape(replica_rows, cache_size, heads_here, HD)
    scale = HD ** (-0.5)
    cache_score = (
        jnp.einsum("srkgd,rpkd->srkgp", query_all, cache_keys, preferred_element_type=jnp.float32)
        * scale
    )
    valid = jnp.arange(cache_size)[None, :] < cache_len[:, None]
    cache_score = jnp.where(valid[None, :, None, None, :], cache_score, neg_fill)
    fresh_score = (
        jnp.einsum("srkgd,trkd->srkgt", query_all, newkey_all, preferred_element_type=jnp.float32)
        * scale
    )
    causal = jnp.arange(STEPS)[:, None] >= jnp.arange(STEPS)[None, :]
    fresh_score = jnp.where(causal[:, None, None, None, :], fresh_score, neg_fill)
    top = jnp.maximum(jnp.max(cache_score, axis=-1), jnp.max(fresh_score, axis=-1))
    cache_exp = jnp.exp(cache_score - top[..., None])
    fresh_exp = jnp.exp(fresh_score - top[..., None])
    total = jnp.sum(cache_exp, axis=-1) + jnp.sum(fresh_exp, axis=-1)
    cache_wts = (cache_exp / total[..., None]).astype(jnp.bfloat16)
    fresh_wts = (fresh_exp / total[..., None]).astype(jnp.bfloat16)
    output = jnp.einsum(
        "srkgp,rpkd->srkgd", cache_wts, cache_vals, preferred_element_type=jnp.float32
    )
    output = output + jnp.einsum(
        "srkgt,trkd->srkgd", fresh_wts, values, preferred_element_type=jnp.float32
    )
    decoded = output.astype(jnp.bfloat16).reshape(STEPS * replica_rows, heads_here * share * HD)
    result = jnp.where(is_learner, learner_rows, decoded)
    return result[None]


def solution(mesh):
    roles, dp, tp = (mesh.shape[name] for name in ("role", "dp", "tp"))
    x_size = tp // 2
    fine = Mesh(
        mesh.devices.reshape(roles, x_size, dp // (2 * x_size), 2, x_size, 2),
        ("role", *DP, *TP),
    )
    return jax.shard_map(
        local,
        mesh=fine,
        in_specs=(
            P("role", DP, None),
            P(DP, TP),
            P(DP, TP),
            P(DP, TP),
            P(DP, TP),
            P(None, DP, TP),
            P(None, DP, TP),
            P(DP, None, TP),
            P(DP, None, TP),
            P(DP),
        ),
        out_specs=P("role", DP, TP),
        check_vma=False,
    )
```

```python
import jax
import jax.numpy as jnp
from jax import lax
from jax.experimental import pallas as pl
from jax.experimental.pallas import tpu as pltpu
from jax.sharding import Mesh, PartitionSpec as P


D = 8192
KVH = 8
QH = 64
HD = 128
STEPS = 8


beta_one = 0.9
beta_two = 0.95
adam_eps = 1e-08
bias_one = 1.0 - 0.9**10
bias_two = 1.0 - 0.95**10
neg_fill = -1e30


INTERPRET = False

DP = ("zh", "zl", "yl")
TP = ("x", "core")
NEAR = ("zl", "yl")


def adam_fresh(master, moment1, moment2, gradient):
    step_size = 2.0 * D ** (-0.5)
    first = beta_one * moment1 + (1.0 - beta_one) * gradient
    second = beta_two * moment2 + (1.0 - beta_two) * gradient * gradient
    change = first / bias_one / (jnp.sqrt(second / bias_two) + adam_eps)
    return (master - step_size * change).astype(jnp.bfloat16)


def exchange(value, axis):
    return lax.all_to_all(value, axis, 0, 0, tiled=True)


def gather(value, axis):
    peers = lax.axis_size(axis)
    return exchange(jnp.broadcast_to(value[None], (peers, *value.shape)), axis)


def swap(value, axis, by=1):
    peers = lax.axis_size(axis)
    return lax.ppermute(value, axis, [(i, i ^ by) for i in range(peers)])


def ordered(value, met, first):
    return jnp.where(first, value, met), jnp.where(first, met, value)


def far_shift(value, by, from_role, to_role):
    far = lax.axis_size("zh")
    pairs = [(from_role * far + i, to_role * far + (i + by) % far) for i in range(far)]
    return lax.ppermute(value, ("role", "zh"), pairs)


def far_order(far):
    return sorted(range(far), key=lambda k: -min(k, far - k))


def by_source(received):
    far = len(received)
    back = [received[-m % far] for m in range(far)]
    return lax.dynamic_slice_in_dim(jnp.stack(back + back), -lax.axis_index("zh") % far, far, 0)


def at_index(value, index):
    return lax.dynamic_index_in_dim(value, index, 0, keepdims=False)


def dot32(a, b, dims):
    return lax.dot_general(a, b, (dims, ((), ())), preferred_element_type=jnp.float32)


def value_terms(at_ref, mine_ref, other_ref, *refs):
    parts, (stays_ref, leaves_ref) = refs[:-2], refs[-2:]
    far = len(parts)
    zh_at, first = at_ref[0], at_ref[1] == 0
    line, _, half, width = stays_ref.shape
    step = max(line // 2, 1)
    for slot, rows_ref in enumerate((mine_ref, other_ref)):
        for begin in range(0, line, step):
            rows = pl.ds(begin * 2 * half, step * 2 * half)
            total = None
            for k, part in enumerate(parts):
                f = lax.rem(zh_at - k + far, far)
                term = jnp.dot(rows_ref[f, rows, :], part[...], preferred_element_type=jnp.float32)
                total = term if total is None else total + term
            total = total.reshape(step, 2, half, width)
            low, high = total[:, 0], total[:, 1]
            stays_ref[pl.ds(begin, step), slot] = jnp.where(first, low, high)
            leaves_ref[pl.ds(begin, step), slot] = jnp.where(first, high, low).astype(jnp.bfloat16)


def local(
    hidden, out_grad, master, moment1, moment2, queries, new_keys, k_cache, v_cache, cache_len
):
    is_learner = lax.axis_index("role") == 0
    x_at, core_at = lax.axis_index("x"), lax.axis_index("core")
    zh_at, yl_at = lax.axis_index("zh"), lax.axis_index("yl")
    far, line = lax.axis_size("zh"), lax.axis_size("zl")
    near = line * 2
    tokens, block = hidden.shape[1], master.shape[0]
    half = tokens // 2
    width_here = out_grad.shape[1]
    heads_here = width_here // HD
    share = QH // KVH
    replica_rows = cache_len.shape[0]
    cache_size = k_cache.shape[1]

    mine = lax.dynamic_slice(hidden[0], (core_at * half, x_at * near * block), (half, near * block))
    mine = mine.reshape(half, near, block).transpose(1, 0, 2)
    mine = exchange(mine, NEAR)
    mine, old_weight = lax.optimization_barrier((mine, master.astype(jnp.bfloat16)))
    mine = gather(mine.reshape(near * half, block), "x")
    other = swap(mine, "core")

    by, grads, at = line // 2, out_grad, 0
    while by:
        first = lax.axis_index("zl") & by == 0
        met = swap(grads, "zl", by)
        grads = jnp.stack(ordered(grads, met, first), axis=at)
        by, at = by // 2, at + 1
    grads = jnp.stack(ordered(grads, swap(grads, "yl"), yl_at == 0), axis=at)
    grads = grads.reshape(near, tokens, width_here)
    at_mine, at_other = (
        lax.dynamic_slice(grads, (0, at * half, 0), (near, half, width_here)).reshape(near * half, width_here)
        for at in (core_at, 1 - core_at)
    )

    old_parts = {k: far_shift(old_weight, k, 1, 0) for k in far_order(far)[:-1]}
    old_parts[0] = old_weight

    partial = jnp.stack(
        [
            dot32(mine[f], at_mine, ((0,), (0,))) + dot32(other[f], at_other, ((0,), (0,)))
            for f in range(far)
        ]
    ).astype(jnp.bfloat16)
    gradient = exchange(partial, "zh")

    _, *old_parts = lax.optimization_barrier((partial, *(old_parts[k] for k in range(far))))
    old_weight = by_source(old_parts)
    kept, sent = (
        jnp.stack([dot32(rows, old_weight[f], ((1,), (1,))).astype(jnp.bfloat16) for f in range(far)])
        for rows in (at_mine, at_other)
    )
    back = (kept.astype(jnp.float32) + swap(sent, "core").astype(jnp.float32)).astype(jnp.bfloat16)
    gradient, back = lax.optimization_barrier((gradient, back))

    fresh = adam_fresh(master, moment1, moment2, jnp.sum(gradient.astype(jnp.float32), axis=0))
    parts = {k: far_shift(fresh, k, 0, 1) for k in far_order(far)}
    parts = [parts[k] for k in range(far)]

    back = exchange(back, "x")
    back = jnp.sum(back.astype(jnp.float32), axis=0).astype(jnp.bfloat16)
    back = back.reshape(line, 2, half, block)

    parts, back = lax.optimization_barrier((parts, back))
    shape = (line, 2, half, width_here)
    stays, leaves = pl.pallas_call(
        value_terms,
        out_shape=(
            jax.ShapeDtypeStruct(shape, jnp.float32),
            jax.ShapeDtypeStruct(shape, jnp.bfloat16),
        ),
        in_specs=[pl.BlockSpec(memory_space=pltpu.SMEM)]
        + [pl.BlockSpec(memory_space=pltpu.VMEM)] * (2 + far),
        out_specs=[pl.BlockSpec(memory_space=pltpu.VMEM)] * 2,
        cost_estimate=pl.CostEstimate(
            flops=4 * far * near * half * block * width_here,
            bytes_accessed=4 * far * near * half * block,
            transcendentals=0,
        ),
        interpret=INTERPRET,
    )(jnp.stack([zh_at, yl_at]), mine, other, *parts)
    met = swap(jnp.where(is_learner, back, leaves), "yl")
    back = jnp.stack(
        ordered(
            lax.dynamic_index_in_dim(back, yl_at, 1, keepdims=False),
            lax.dynamic_index_in_dim(met, yl_at, 1, keepdims=False),
            yl_at == 0,
        ),
        axis=1,
    )
    terms = (stays + met.astype(jnp.float32)).astype(jnp.bfloat16)
    moved = exchange(jnp.where(is_learner, back, terms), "zl")
    values = jnp.sum(moved.astype(jnp.float32), axis=0)
    values = jnp.concatenate(ordered(values[0], values[1], core_at == 0))
    back = moved.reshape(2, near // 2, half, block)
    stays, leaves = at_index(back, core_at), at_index(back, 1 - core_at)
    learner_rows = jnp.concatenate(ordered(stays, swap(leaves, "core"), core_at == 0), axis=1)
    learner_rows = learner_rows.transpose(1, 0, 2).reshape(tokens, near // 2 * block)

    values = values.astype(jnp.bfloat16).reshape(STEPS, replica_rows, heads_here, HD)
    query_all = queries.reshape(STEPS, replica_rows, heads_here, share, HD)
    newkey_all = new_keys.reshape(STEPS, replica_rows, heads_here, HD)
    cache_keys = k_cache.reshape(replica_rows, cache_size, heads_here, HD)
    cache_vals = v_cache.reshape(replica_rows, cache_size, heads_here, HD)
    scale = HD ** (-0.5)
    cache_score = (
        jnp.einsum("srkgd,rpkd->srkgp", query_all, cache_keys, preferred_element_type=jnp.float32)
        * scale
    )
    valid = jnp.arange(cache_size)[None, :] < cache_len[:, None]
    cache_score = jnp.where(valid[None, :, None, None, :], cache_score, neg_fill)
    fresh_score = (
        jnp.einsum("srkgd,trkd->srkgt", query_all, newkey_all, preferred_element_type=jnp.float32)
        * scale
    )
    causal = jnp.arange(STEPS)[:, None] >= jnp.arange(STEPS)[None, :]
    fresh_score = jnp.where(causal[:, None, None, None, :], fresh_score, neg_fill)
    top = jnp.maximum(jnp.max(cache_score, axis=-1), jnp.max(fresh_score, axis=-1))
    cache_exp = jnp.exp(cache_score - top[..., None])
    fresh_exp = jnp.exp(fresh_score - top[..., None])
    total = jnp.sum(cache_exp, axis=-1) + jnp.sum(fresh_exp, axis=-1)
    cache_wts = (cache_exp / total[..., None]).astype(jnp.bfloat16)
    fresh_wts = (fresh_exp / total[..., None]).astype(jnp.bfloat16)
    output = jnp.einsum(
        "srkgp,rpkd->srkgd", cache_wts, cache_vals, preferred_element_type=jnp.float32
    )
    output = output + jnp.einsum(
        "srkgt,trkd->srkgd", fresh_wts, values, preferred_element_type=jnp.float32
    )
    decoded = output.astype(jnp.bfloat16).reshape(STEPS * replica_rows, heads_here * share * HD)
    result = jnp.where(is_learner, learner_rows, decoded)
    return result[None]


def solution(mesh):
    roles, dp, tp = (mesh.shape[name] for name in ("role", "dp", "tp"))
    x_size = tp // 2
    fine = Mesh(
        mesh.devices.reshape(roles, x_size, dp // (2 * x_size), 2, x_size, 2),
        ("role", *DP, *TP),
    )
    return jax.shard_map(
        local,
        mesh=fine,
        in_specs=(
            P("role", DP, None),
            P(DP, TP),
            P(DP, TP),
            P(DP, TP),
            P(DP, TP),
            P(None, DP, TP),
            P(None, DP, TP),
            P(DP, None, TP),
            P(DP, None, TP),
            P(DP),
        ),
        out_specs=P("role", DP, TP),
        check_vma=False,
    )
```

```python
import jax
import jax.numpy as jnp
from jax import lax
from jax.experimental import pallas as pl
from jax.experimental.pallas import tpu as pltpu
from jax.sharding import Mesh, PartitionSpec as P


D = 8192
KVH = 8
QH = 64
HD = 128
STEPS = 8


beta_one = 0.9
beta_two = 0.95
adam_eps = 1e-08
bias_one = 1.0 - 0.9**10
bias_two = 1.0 - 0.95**10
neg_fill = -1e30


INTERPRET = False

DP = ("zh", "zl", "yl")
TP = ("x", "core")
NEAR = ("zl", "yl")


def adam_fresh(master, moment1, moment2, gradient):
    step_size = 2.0 * D ** (-0.5)
    first = beta_one * moment1 + (1.0 - beta_one) * gradient
    second = beta_two * moment2 + (1.0 - beta_two) * gradient * gradient
    change = first / bias_one / (jnp.sqrt(second / bias_two) + adam_eps)
    return (master - step_size * change).astype(jnp.bfloat16)


def exchange(value, axis):
    return lax.all_to_all(value, axis, 0, 0, tiled=True)


def gather(value, axis):
    peers = lax.axis_size(axis)
    return exchange(jnp.broadcast_to(value[None], (peers, *value.shape)), axis)


def swap(value, axis, by=1):
    peers = lax.axis_size(axis)
    return lax.ppermute(value, axis, [(i, i ^ by) for i in range(peers)])


def ordered(value, met, first):
    return jnp.where(first, value, met), jnp.where(first, met, value)


def far_shift(value, by, from_role, to_role):
    far = lax.axis_size("zh")
    pairs = [(from_role * far + i, to_role * far + (i + by) % far) for i in range(far)]
    return lax.ppermute(value, ("role", "zh"), pairs)


def far_order(far):
    return sorted(range(far), key=lambda k: -min(k, far - k))


def at_index(value, index):
    return lax.dynamic_index_in_dim(value, index, 0, keepdims=False)


def dot32(a, b, dims):
    return lax.dot_general(a, b, (dims, ((), ())), preferred_element_type=jnp.float32)


def back_terms(at_ref, mine_ref, other_ref, *refs):
    parts, outs = refs[:-2], refs[-2:]
    far = len(parts)

    @pl.when(at_ref[0] == 0)
    def _():
        for k, part in enumerate(parts):
            f = lax.rem(at_ref[1] - k + far, far)
            for rows, out in zip((mine_ref, other_ref), outs):
                out[f] = dot32(rows[...], part[...], ((1,), (1,))).astype(jnp.bfloat16)


def before_swap(at_ref, mine_ref, other_ref, back_ref, *refs):
    parts, (stays_ref, sent_ref) = refs[:-2], refs[-2:]
    far = len(parts)
    zh_at, first = at_ref[1], at_ref[2] == 0
    line, _, half, width = stays_ref.shape
    step = max(line // 2, 1)

    @pl.when(at_ref[0] == 0)
    def _():
        for begin in range(0, line, step):
            rows = pl.ds(begin * 2 * half, step * 2 * half)
            total = sum(back_ref[i, rows, :].astype(jnp.float32) for i in range(far))
            sent_ref[pl.ds(begin, step)] = total.astype(jnp.bfloat16).reshape(step, 2, half, width)

    @pl.when(at_ref[0] == 1)
    def _():
        for slot, rows_ref in enumerate((mine_ref, other_ref)):
            for begin in range(0, line, step):
                rows = pl.ds(begin * 2 * half, step * 2 * half)
                total = None
                for k, part in enumerate(parts):
                    f = lax.rem(zh_at - k + far, far)
                    term = dot32(rows_ref[f, rows, :], part[...], ((1,), (0,)))
                    total = term if total is None else total + term
                total = total.reshape(step, 2, half, width)
                low, high = total[:, 0], total[:, 1]
                stays_ref[pl.ds(begin, step), slot] = jnp.where(first, low, high)
                sent_ref[pl.ds(begin, step), slot] = jnp.where(first, high, low).astype(jnp.bfloat16)


def after_swap(at_ref, own_ref, met_ref, stays_ref, out_ref):
    @pl.when(at_ref[0] == 1)
    def _():
        out_ref[...] = (stays_ref[...] + met_ref[...].astype(jnp.float32)).astype(jnp.bfloat16)

    @pl.when((at_ref[0] == 0) & (at_ref[2] == 0))
    def _():
        out_ref[:, 0] = own_ref[:, 0]
        out_ref[:, 1] = met_ref[:, 0]

    @pl.when((at_ref[0] == 0) & (at_ref[2] == 1))
    def _():
        out_ref[:, 0] = met_ref[:, 1]
        out_ref[:, 1] = own_ref[:, 1]


def in_vmem(kernel, outs, flops, at, *args):
    vmem = pl.BlockSpec(memory_space=pltpu.VMEM)
    many = isinstance(outs, tuple)
    moved = sum(v.size * v.dtype.itemsize for v in (*args, *(outs if many else (outs,))))
    return pl.pallas_call(
        kernel,
        out_shape=outs,
        in_specs=[pl.BlockSpec(memory_space=pltpu.SMEM)] + [vmem] * len(args),
        out_specs=(vmem,) * len(outs) if many else vmem,
        cost_estimate=pl.CostEstimate(flops=flops, bytes_accessed=moved, transcendentals=0),
        interpret=INTERPRET,
    )(at, *args)


def local(
    hidden, out_grad, master, moment1, moment2, queries, new_keys, k_cache, v_cache, cache_len
):
    is_learner = lax.axis_index("role") == 0
    x_at, core_at = lax.axis_index("x"), lax.axis_index("core")
    zh_at, yl_at = lax.axis_index("zh"), lax.axis_index("yl")
    far, line = lax.axis_size("zh"), lax.axis_size("zl")
    near = line * 2
    tokens, block = hidden.shape[1], master.shape[0]
    half = tokens // 2
    width_here = out_grad.shape[1]
    heads_here = width_here // HD
    share = QH // KVH
    replica_rows = cache_len.shape[0]
    cache_size = k_cache.shape[1]

    mine = lax.dynamic_slice(hidden[0], (core_at * half, x_at * near * block), (half, near * block))
    mine = mine.reshape(half, near, block).transpose(1, 0, 2)
    mine = exchange(mine, NEAR)
    mine, old_weight = lax.optimization_barrier((mine, master.astype(jnp.bfloat16)))
    mine = gather(mine.reshape(near * half, block), "x")
    other = swap(mine, "core")

    by, grads, at = line // 2, out_grad, 0
    while by:
        first = lax.axis_index("zl") & by == 0
        met = swap(grads, "zl", by)
        grads = jnp.stack(ordered(grads, met, first), axis=at)
        by, at = by // 2, at + 1
    grads = jnp.stack(ordered(grads, swap(grads, "yl"), yl_at == 0), axis=at)
    grads = grads.reshape(near, tokens, width_here)
    at_mine, at_other = (
        lax.dynamic_slice(grads, (0, at * half, 0), (near, half, width_here)).reshape(near * half, width_here)
        for at in (core_at, 1 - core_at)
    )

    old_parts = {k: far_shift(old_weight, k, 1, 0) for k in far_order(far)[:-1]}
    old_parts[0] = old_weight

    partial = jnp.stack(
        [
            dot32(mine[f], at_mine, ((0,), (0,))) + dot32(other[f], at_other, ((0,), (0,)))
            for f in range(far)
        ]
    ).astype(jnp.bfloat16)
    gradient = at_index(partial, zh_at).astype(jnp.float32)
    for k in far_order(far)[:-1]:
        gradient += far_shift(at_index(partial, (zh_at + k) % far), k, 0, 0).astype(jnp.float32)

    fresh = adam_fresh(master, moment1, moment2, gradient)
    parts = {k: far_shift(fresh, k, 0, 1) for k in far_order(far)}

    at = jnp.stack([lax.axis_index("role"), zh_at, yl_at])
    flops = 4 * far * near * half * block * width_here
    wide = jax.ShapeDtypeStruct((far, near * half, block), jnp.bfloat16)
    kept, sent = in_vmem(
        back_terms, (wide, wide), flops, at, at_mine, at_other, *(old_parts[k] for k in range(far))
    )
    back = (kept.astype(jnp.float32) + swap(sent, "core").astype(jnp.float32)).astype(jnp.bfloat16)
    back = exchange(back, "x")

    shape = (line, 2, half, width_here)
    narrow = jax.ShapeDtypeStruct(shape, jnp.bfloat16)
    stays, own = in_vmem(
        before_swap,
        (jax.ShapeDtypeStruct(shape, jnp.float32), narrow),
        flops, at, mine, other, back, *(parts[k] for k in range(far)),
    )
    last = in_vmem(after_swap, narrow, 0, at, own, swap(own, "yl"), stays)
    moved = exchange(last, "zl")
    values = jnp.sum(moved.astype(jnp.float32), axis=0)
    values = jnp.concatenate(ordered(values[0], values[1], core_at == 0))
    back = moved.reshape(2, near // 2, half, block)
    stays, leaves = at_index(back, core_at), at_index(back, 1 - core_at)
    learner_rows = jnp.concatenate(ordered(stays, swap(leaves, "core"), core_at == 0), axis=1)
    learner_rows = learner_rows.transpose(1, 0, 2).reshape(tokens, near // 2 * block)

    values = values.astype(jnp.bfloat16).reshape(STEPS, replica_rows, heads_here, HD)
    query_all = queries.reshape(STEPS, replica_rows, heads_here, share, HD)
    newkey_all = new_keys.reshape(STEPS, replica_rows, heads_here, HD)
    cache_keys = k_cache.reshape(replica_rows, cache_size, heads_here, HD)
    cache_vals = v_cache.reshape(replica_rows, cache_size, heads_here, HD)
    scale = HD ** (-0.5)
    cache_score = (
        jnp.einsum("srkgd,rpkd->srkgp", query_all, cache_keys, preferred_element_type=jnp.float32)
        * scale
    )
    valid = jnp.arange(cache_size)[None, :] < cache_len[:, None]
    cache_score = jnp.where(valid[None, :, None, None, :], cache_score, neg_fill)
    fresh_score = (
        jnp.einsum("srkgd,trkd->srkgt", query_all, newkey_all, preferred_element_type=jnp.float32)
        * scale
    )
    causal = jnp.arange(STEPS)[:, None] >= jnp.arange(STEPS)[None, :]
    fresh_score = jnp.where(causal[:, None, None, None, :], fresh_score, neg_fill)
    top = jnp.maximum(jnp.max(cache_score, axis=-1), jnp.max(fresh_score, axis=-1))
    cache_exp = jnp.exp(cache_score - top[..., None])
    fresh_exp = jnp.exp(fresh_score - top[..., None])
    total = jnp.sum(cache_exp, axis=-1) + jnp.sum(fresh_exp, axis=-1)
    cache_wts = (cache_exp / total[..., None]).astype(jnp.bfloat16)
    fresh_wts = (fresh_exp / total[..., None]).astype(jnp.bfloat16)
    output = jnp.einsum(
        "srkgp,rpkd->srkgd", cache_wts, cache_vals, preferred_element_type=jnp.float32
    )
    output = output + jnp.einsum(
        "srkgt,trkd->srkgd", fresh_wts, values, preferred_element_type=jnp.float32
    )
    decoded = output.astype(jnp.bfloat16).reshape(STEPS * replica_rows, heads_here * share * HD)
    result = jnp.where(is_learner, learner_rows, decoded)
    return result[None]


def solution(mesh):
    roles, dp, tp = (mesh.shape[name] for name in ("role", "dp", "tp"))
    x_size = tp // 2
    fine = Mesh(
        mesh.devices.reshape(roles, x_size, dp // (2 * x_size), 2, x_size, 2),
        ("role", *DP, *TP),
    )
    return jax.shard_map(
        local,
        mesh=fine,
        in_specs=(
            P("role", DP, None),
            P(DP, TP),
            P(DP, TP),
            P(DP, TP),
            P(DP, TP),
            P(None, DP, TP),
            P(None, DP, TP),
            P(DP, None, TP),
            P(DP, None, TP),
            P(DP),
        ),
        out_specs=P("role", DP, TP),
        check_vma=False,
    )
```

```python
import jax
import jax.numpy as jnp
from jax import lax
from jax.experimental import pallas as pl
from jax.experimental.pallas import tpu as pltpu
from jax.sharding import Mesh, PartitionSpec as P


D = 8192
KVH = 8
QH = 64
HD = 128
STEPS = 8


beta_one = 0.9
beta_two = 0.95
adam_eps = 1e-08
bias_one = 1.0 - 0.9**10
bias_two = 1.0 - 0.95**10
neg_fill = -1e30


INTERPRET = False

DP = ("zh", "zl", "yl")
TP = ("x", "core")
NEAR = ("zl", "yl")


def adam_fresh(master, moment1, moment2, gradient):
    step_size = 2.0 * D ** (-0.5)
    first = beta_one * moment1 + (1.0 - beta_one) * gradient
    second = beta_two * moment2 + (1.0 - beta_two) * gradient * gradient
    change = first / bias_one / (jnp.sqrt(second / bias_two) + adam_eps)
    return (master - step_size * change).astype(jnp.bfloat16)


def exchange(value, axis):
    return lax.all_to_all(value, axis, 0, 0, tiled=True)


def gather(value, axis):
    peers = lax.axis_size(axis)
    return exchange(jnp.broadcast_to(value[None], (peers, *value.shape)), axis)


def swap(value, axis, by=1):
    peers = lax.axis_size(axis)
    return lax.ppermute(value, axis, [(i, i ^ by) for i in range(peers)])


def ordered(value, met, first):
    return jnp.where(first, value, met), jnp.where(first, met, value)


def far_shift(value, by, from_role, to_role):
    far = lax.axis_size("zh")
    pairs = [(from_role * far + i, to_role * far + (i + by) % far) for i in range(far)]
    return lax.ppermute(value, ("role", "zh"), pairs)


def far_order(far):
    return sorted(range(far), key=lambda k: -min(k, far - k))


def at_index(value, index):
    return lax.dynamic_index_in_dim(value, index, 0, keepdims=False)


def dot32(a, b, dims):
    return lax.dot_general(a, b, (dims, ((), ())), preferred_element_type=jnp.float32)


def back_terms(at_ref, mine_ref, other_ref, *refs):
    parts, outs = refs[:-2], refs[-2:]
    far = len(parts)

    @pl.when(at_ref[0] == 0)
    def _():
        for k, part in enumerate(parts):
            f = lax.rem(at_ref[1] - k + far, far)
            for rows, out in zip((mine_ref, other_ref), outs):
                out[f] = dot32(rows[...], part[...], ((1,), (1,))).astype(jnp.bfloat16)


def before_swap(at_ref, mine_ref, other_ref, back_ref, *refs):
    parts, (stays_ref, sent_ref) = refs[:-2], refs[-2:]
    far = len(parts)
    zh_at, first = at_ref[1], at_ref[2] == 0
    line, _, half, width = stays_ref.shape
    step = max(line // 2, 1)

    @pl.when(at_ref[0] == 0)
    def _():
        for begin in range(0, line, step):
            rows = pl.ds(begin * 2 * half, step * 2 * half)
            total = sum(back_ref[i, rows, :].astype(jnp.float32) for i in range(far))
            sent_ref[pl.ds(begin, step)] = total.astype(jnp.bfloat16).reshape(step, 2, half, width)

    @pl.when(at_ref[0] == 1)
    def _():
        for slot, rows_ref in enumerate((mine_ref, other_ref)):
            for begin in range(0, line, step):
                rows = pl.ds(begin * 2 * half, step * 2 * half)
                total = None
                for k, part in enumerate(parts):
                    f = lax.rem(zh_at - k + far, far)
                    term = dot32(rows_ref[f, rows, :], part[...], ((1,), (0,)))
                    total = term if total is None else total + term
                total = total.reshape(step, 2, half, width)
                low, high = total[:, 0], total[:, 1]
                stays_ref[pl.ds(begin, step), slot] = jnp.where(first, low, high)
                sent_ref[pl.ds(begin, step), slot] = jnp.where(first, high, low).astype(jnp.bfloat16)


def after_swap(at_ref, own_ref, met_ref, stays_ref, out_ref):
    @pl.when(at_ref[0] == 1)
    def _():
        out_ref[...] = (stays_ref[...] + met_ref[...].astype(jnp.float32)).astype(jnp.bfloat16)

    @pl.when((at_ref[0] == 0) & (at_ref[2] == 0))
    def _():
        out_ref[:, 0] = own_ref[:, 0]
        out_ref[:, 1] = met_ref[:, 0]

    @pl.when((at_ref[0] == 0) & (at_ref[2] == 1))
    def _():
        out_ref[:, 0] = met_ref[:, 1]
        out_ref[:, 1] = own_ref[:, 1]


def in_vmem(kernel, outs, flops, at, *args):
    vmem = pl.BlockSpec(memory_space=pltpu.VMEM)
    many = isinstance(outs, tuple)
    moved = sum(v.size * v.dtype.itemsize for v in (*args, *(outs if many else (outs,))))
    return pl.pallas_call(
        kernel,
        out_shape=outs,
        in_specs=[pl.BlockSpec(memory_space=pltpu.SMEM)] + [vmem] * len(args),
        out_specs=(vmem,) * len(outs) if many else vmem,
        cost_estimate=pl.CostEstimate(flops=flops, bytes_accessed=moved, transcendentals=0),
        interpret=INTERPRET,
    )(at, *args)


def local(
    hidden, out_grad, master, moment1, moment2, queries, new_keys, k_cache, v_cache, cache_len
):
    is_learner = lax.axis_index("role") == 0
    x_at, core_at = lax.axis_index("x"), lax.axis_index("core")
    zh_at, yl_at = lax.axis_index("zh"), lax.axis_index("yl")
    far, line = lax.axis_size("zh"), lax.axis_size("zl")
    near = line * 2
    tokens, block = hidden.shape[1], master.shape[0]
    half = tokens // 2
    width_here = out_grad.shape[1]
    heads_here = width_here // HD
    share = QH // KVH
    replica_rows = cache_len.shape[0]
    cache_size = k_cache.shape[1]

    mine = lax.dynamic_slice(hidden[0], (core_at * half, x_at * near * block), (half, near * block))
    mine = mine.reshape(half, near, block).transpose(1, 0, 2)
    mine = exchange(mine, NEAR)
    mine, old_weight = lax.optimization_barrier((mine, master.astype(jnp.bfloat16)))
    mine = gather(mine.reshape(near * half, block), "x")
    other = swap(mine, "core")

    by, grads, at = line // 2, out_grad, 0
    while by:
        first = lax.axis_index("zl") & by == 0
        met = swap(grads, "zl", by)
        grads = jnp.stack(ordered(grads, met, first), axis=at)
        by, at = by // 2, at + 1
    met = swap(grads, "yl")
    grads = jnp.stack(ordered(grads, met, yl_at == 0), axis=at)
    grads = grads.reshape(near, tokens, width_here)
    at_mine, at_other = (
        lax.dynamic_slice(grads, (0, at * half, 0), (near, half, width_here)).reshape(near * half, width_here)
        for at in (core_at, 1 - core_at)
    )

    old_parts = {k: far_shift(old_weight, k, 1, 0) for k in far_order(far)[:-1]}
    old_parts[0] = old_weight

    partial = jnp.stack(
        [
            dot32(mine[f], at_mine, ((0,), (0,))) + dot32(other[f], at_other, ((0,), (0,)))
            for f in range(far)
        ]
    ).astype(jnp.bfloat16)
    gradient = [at_index(partial, zh_at)] + [
        far_shift(at_index(partial, (zh_at + k) % far), k, 0, 0)
        for k in far_order(far)[:-1]
    ]

    at = jnp.stack([lax.axis_index("role"), zh_at, yl_at])
    flops = 4 * far * near * half * block * width_here
    wide = jax.ShapeDtypeStruct((far, near * half, block), jnp.bfloat16)
    kept, sent = in_vmem(
        back_terms, (wide, wide), flops, at, at_mine, at_other, *(old_parts[k] for k in range(far))
    )
    back = (kept.astype(jnp.float32) + swap(sent, "core").astype(jnp.float32)).astype(jnp.bfloat16)
    gradient, _ = lax.optimization_barrier((gradient, back))
    back = exchange(back, "x")


    fresh = adam_fresh(master, moment1, moment2, sum(g.astype(jnp.float32) for g in gradient))
    parts = {k: far_shift(fresh, k, 0, 1) for k in far_order(far)}

    shape = (line, 2, half, width_here)
    narrow = jax.ShapeDtypeStruct(shape, jnp.bfloat16)
    stays, own = in_vmem(
        before_swap,
        (jax.ShapeDtypeStruct(shape, jnp.float32), narrow),
        flops, at, mine, other, back, *(parts[k] for k in range(far)),
    )
    last = in_vmem(after_swap, narrow, 0, at, own, swap(own, "yl"), stays)
    moved = exchange(last, "zl")
    values = jnp.sum(moved.astype(jnp.float32), axis=0)
    values = jnp.concatenate(ordered(values[0], values[1], core_at == 0))
    back = moved.reshape(2, near // 2, half, block)
    stays, leaves = at_index(back, core_at), at_index(back, 1 - core_at)
    learner_rows = jnp.concatenate(ordered(stays, swap(leaves, "core"), core_at == 0), axis=1)
    learner_rows = learner_rows.transpose(1, 0, 2).reshape(tokens, near // 2 * block)

    values = values.astype(jnp.bfloat16).reshape(STEPS, replica_rows, heads_here, HD)
    query_all = queries.reshape(STEPS, replica_rows, heads_here, share, HD)
    newkey_all = new_keys.reshape(STEPS, replica_rows, heads_here, HD)
    cache_keys = k_cache.reshape(replica_rows, cache_size, heads_here, HD)
    cache_vals = v_cache.reshape(replica_rows, cache_size, heads_here, HD)
    scale = HD ** (-0.5)
    cache_score = (
        jnp.einsum("srkgd,rpkd->srkgp", query_all, cache_keys, preferred_element_type=jnp.float32)
        * scale
    )
    valid = jnp.arange(cache_size)[None, :] < cache_len[:, None]
    cache_score = jnp.where(valid[None, :, None, None, :], cache_score, neg_fill)
    fresh_score = (
        jnp.einsum("srkgd,trkd->srkgt", query_all, newkey_all, preferred_element_type=jnp.float32)
        * scale
    )
    causal = jnp.arange(STEPS)[:, None] >= jnp.arange(STEPS)[None, :]
    fresh_score = jnp.where(causal[:, None, None, None, :], fresh_score, neg_fill)
    top = jnp.maximum(jnp.max(cache_score, axis=-1), jnp.max(fresh_score, axis=-1))
    cache_exp = jnp.exp(cache_score - top[..., None])
    fresh_exp = jnp.exp(fresh_score - top[..., None])
    total = jnp.sum(cache_exp, axis=-1) + jnp.sum(fresh_exp, axis=-1)
    cache_wts = (cache_exp / total[..., None]).astype(jnp.bfloat16)
    fresh_wts = (fresh_exp / total[..., None]).astype(jnp.bfloat16)
    output = jnp.einsum(
        "srkgp,rpkd->srkgd", cache_wts, cache_vals, preferred_element_type=jnp.float32
    )
    output = output + jnp.einsum(
        "srkgt,trkd->srkgd", fresh_wts, values, preferred_element_type=jnp.float32
    )
    decoded = output.astype(jnp.bfloat16).reshape(STEPS * replica_rows, heads_here * share * HD)
    result = jnp.where(is_learner, learner_rows, decoded)
    return result[None]


def solution(mesh):
    roles, dp, tp = (mesh.shape[name] for name in ("role", "dp", "tp"))
    x_size = tp // 2
    fine = Mesh(
        mesh.devices.reshape(roles, x_size, dp // (2 * x_size), 2, x_size, 2),
        ("role", *DP, *TP),
    )
    return jax.shard_map(
        local,
        mesh=fine,
        in_specs=(
            P("role", DP, None),
            P(DP, TP),
            P(DP, TP),
            P(DP, TP),
            P(DP, TP),
            P(None, DP, TP),
            P(None, DP, TP),
            P(DP, None, TP),
            P(DP, None, TP),
            P(DP),
        ),
        out_specs=P("role", DP, TP),
        check_vma=False,
    )
```
